512 devices in a mesh: flow: 16 (over y_lo, x, core), tm: 32 (over z, y_hi).
Axes of the slice: x: 4, y: 4 (y_hi: 2, y_lo: 2; y = y_hi * 2 + y_lo), z: 16, core: 2. Of those that a mesh axis runs over, the one named last changes fastest.
Arguments:
- frames: bfloat16 [512, 512, 1024], P('tm', 'flow'), may hold values from -6 to 6
- pixel_gain: float32 [512, 1024], P('flow'), may hold values from 0.1 to 1.9
- couple: float32 [512, 1024], P('flow'), may hold values from 0.05 to 0.45
- bin_index: int32 [512, 1024], P('flow'), may hold values from 0 to 31
- pixel_mask: int32 [512, 1024], P('flow'), may hold values 0 or 1
- offsets: int32 [512], P('tm'), may hold values from 0 to 24, as said below
Outputs:
- correlation: float32 [32, 32], P('flow', 'tm')
The draws below stay inside these ranges and needn't reach their ends.
Inputs may be any that keep to these rules, and one draw needn't show every extreme that they name: The pixels of frame t pair with the pixels offsets[t] rows further along the flow in the later frames; the value 24 occurs in every draw.
All inputs are finite; a program needn't handle non-finite values. No bound on the sum of `pixel_mask` on one device may be relied on, other than what follows from the above.
Results may differ from the reference program's by a relative error of at most 0.0041.
Values may be sent and summed in bfloat16 or wider, within the bound.
No kernel may reach another device: no remote copies, remote signals or barrier semaphores. Data moves between devices by JAX's collectives and lax.ppermute only.
A program may use at most 64 MiB of HBM per device.

```python
import jax
import jax.numpy as jnp
from jax import lax

COLS = 1024
LAGS = 32
OFF_MAX = 24
Q = 32
FRAMES = 512
NR = 512


def draw_offsets(key, part):
    key_values, key_top, key_spacing = jax.random.split(key, 3)
    values = jax.random.randint(key_values, (FRAMES,), 0, OFF_MAX + 1, dtype=jnp.int32)
    top_at = jax.random.randint(key_top, (), 0, FRAMES, dtype=jnp.int32)
    spacing = jax.random.randint(key_spacing, (), 1, FRAMES, dtype=jnp.int32)
    low_at = (top_at + spacing) % FRAMES
    values = values.at[top_at].set(OFF_MAX)
    values = values.at[low_at].set(0)
    return values


def touch_ends(values, key, smallest, high):
    spot = [jax.random.randint(jax.random.fold_in(key, axis), (), 0, length) for axis, length in enumerate(values.shape)]
    main_axis = values.shape.index(max(values.shape))
    beside = spot[:main_axis] + [(spot[main_axis] + 1) % values.shape[main_axis]] + spot[main_axis + 1:]
    return values.at[tuple(spot)].set(smallest).at[tuple(beside)].set(high)


def block_scale(rng, shape, pieces, low, top_value):
    gain, own = 1.0, jax.random.fold_in(rng, 6)
    for dim, parts in pieces:
        heights = jnp.exp(jax.random.uniform(jax.random.fold_in(own, dim), (parts,), jnp.float32, low / len(pieces), top_value / len(pieces)))
        gain = gain * jnp.repeat(heights, shape[dim] // parts).reshape([-1 if axis == dim else 1 for axis in range(len(shape))])
    return gain


def scatter_about(key, extent, scale, bound, shards=(), kind=jnp.bfloat16):
    loudness = block_scale(key, extent, shards, -0.22, 0.18) if shards else 1.0
    array = jax.random.normal(key, extent, jnp.float32) * scale * loudness
    return jnp.minimum(jnp.maximum(array, -bound), bound).astype(kind)


def setup_inputs(seed: int = 0) -> dict:
    key_list = jax.random.split(jax.random.key(seed), 7)
    return {
        "frames": scatter_about(key_list[0], (FRAMES, NR, COLS), 1.0, 6.0, ((0, 32), (1, 16))),
        "pixel_gain": jnp.clip(1.0 + 0.18 * jax.random.normal(key_list[1], (NR, COLS), jnp.float32), 0.1, 1.9),
        "couple": jnp.clip(0.05 + 0.39999999 * jax.random.uniform(key_list[2], (NR, COLS), jnp.float32) ** block_scale(key_list[2], (NR, COLS), ((0, 16),), -0.2, 0.2), 0.05, 0.45),
        "bin_index": touch_ends(jax.random.randint(key_list[3], (NR, COLS), 0, Q), jax.random.fold_in(key_list[3], 1), 0, Q - 1).astype(jnp.int32),
        "pixel_mask": touch_ends((jax.random.randint(key_list[4], (NR, COLS), 0, 8) < 7).astype(jnp.int32), jax.random.fold_in(key_list[4], 1), 0, 1),
        "offsets": draw_offsets(jax.random.fold_in(key_list[6], 71), 0),
    }


def correct_one(raw, pixel_gain, couple, mask_float):
    signal = raw.astype(jnp.float32)
    padded = jnp.pad(signal, ((1, 1), (0, 0)))
    return ((pixel_gain * signal + couple * (padded[:-2] + padded[2:])) * mask_float).astype(jnp.bfloat16)

def reference(frames, pixel_gain, couple, bin_index, pixel_mask, offsets):
    mask_float = pixel_mask.astype(jnp.float32)
    corrected = lax.map(lambda raw: correct_one(raw, pixel_gain, couple, mask_float), frames)
    padded = jnp.pad(corrected, ((0, LAGS), (0, OFF_MAX), (0, 0)))

    def add_frame(running, frame_index):
        current = lax.dynamic_index_in_dim(corrected, frame_index, 0, keepdims=False).astype(jnp.float32)
        window = lax.dynamic_slice(padded, (frame_index + 1, offsets[frame_index], jnp.int32(0)), (LAGS, NR, COLS)).astype(jnp.float32)
        return (running + current[None] * window, None)
    running, ignored = lax.scan(add_frame, jnp.zeros((LAGS, NR, COLS), jnp.float32), jnp.arange(FRAMES, dtype=jnp.int32))
    bin_table = (bin_index.reshape(-1)[:, None] == jnp.arange(Q, dtype=jnp.int32)[None, :]).astype(jnp.float32)
    bin_sums = jnp.dot(running.reshape(LAGS, NR * COLS), bin_table, precision=lax.Precision.HIGHEST)
    lag_values = jnp.arange(1, LAGS + 1, dtype=jnp.int32).astype(jnp.float32)
    normaliser = jnp.sqrt((FRAMES - lag_values) * (NR * COLS / Q))
    return bin_sums.T / normaliser[None, :]
```

```python
import jax
import jax.numpy as jnp
from jax import lax
from jax.experimental import pallas as pl
from jax.experimental.pallas import tpu as pltpu
from jax.sharding import PartitionSpec as P

LAGS = 32
OFF_MAX = 24
Q = 32
F32, BF16 = jnp.float32, jnp.bfloat16
VMEM = pl.BlockSpec(memory_space=pltpu.VMEM)
SMEM = pl.BlockSpec(memory_space=pltpu.SMEM)


def correct_kernel(
    h_ref, f_ref, up_ref, dn_ref, gain_ref, couple_ref, mask_ref, o24, o8, t24, t8, raw, done
):
    h = h_ref[0]

    @pl.loop(0, 16)
    def _(f):
        for j in range(8):
            cols = slice(128 * j, 128 * j + 128)
            for k in range(2):
                raw[f, j, 8 + 16 * k : 24 + 16 * k, :] = f_ref[
                    f, 16 * k : 16 * k + 16, cols
                ].astype(F32)

    for f in range(16):
        for j in range(8):
            cols = slice(128 * j, 128 * j + 128)
            raw[f, j, 7:8, :] = up_ref[f : f + 1, cols].astype(F32)
            raw[f, j, 40:41, :] = dn_ref[f : f + 1, cols].astype(F32)

    @pl.loop(0, 16)
    def _(f):
        for j in range(8):
            cols = slice(128 * j, 128 * j + 128)
            for k in range(4):
                rows = slice(8 * k, 8 * k + 8)
                here = raw[f, j, 8 * k + 8 : 8 * k + 16, :]
                above = raw[f, j, 8 * k + 7 : 8 * k + 15, :]
                below = raw[f, j, 8 * k + 9 : 8 * k + 17, :]
                value = gain_ref[rows, cols] * here + couple_ref[rows, cols] * (above + below)
                value = value * mask_ref[rows, cols].astype(F32)
                start = (j // 4) * 2048 + k * 512 + (j % 4) + 4 * f
                done[pl.ds(start, 8, stride=64), :] = value

    own = pl.multiple_of(h * 2048, 2048)
    other = pl.multiple_of(2048 - h * 2048, 2048)

    @pl.loop(0, 24)
    def _(r):
        o24[r] = done[pl.ds(own + r * 64, 64), :].astype(BF16)
        t24[r] = done[pl.ds(other + r * 64, 64), :].astype(BF16)

    @pl.loop(0, 8)
    def _(r):
        o8[r] = done[pl.ds(own + (r + 24) * 64, 64), :].astype(BF16)
        t8[r] = done[pl.ds(other + (r + 24) * 64, 64), :].astype(BF16)


def correct(h, frames, up, dn, gain, couple, mask):
    shapes = tuple(jax.ShapeDtypeStruct((n, 64, 128), BF16) for n in (24, 8, 24, 8))
    return pl.pallas_call(
        correct_kernel,
        out_shape=shapes,
        in_specs=[SMEM] + [VMEM] * 6,
        out_specs=(VMEM,) * 4,
        scratch_shapes=[
            pltpu.VMEM((16, 8, 48, 128), F32),
            pltpu.VMEM((2 * 32 * 64, 128), F32),
        ],
        name="correct",
        cost_estimate=pl.CostEstimate(flops=4000000, bytes_accessed=3000000, transcendentals=0),
        compiler_params=pltpu.CompilerParams(vmem_limit_bytes=16 << 20),
    )(h, frames, up, dn, gain, couple, mask)


def correlate_kernel(h_ref, offo_ref, offr_ref, bins_ref, *refs):
    blocks, (out_ref, later, sums, table, off) = refs[:12], refs[12:]
    h = h_ref[0]
    for k in range(16):
        off[16 * h + k] = offo_ref[k]
        off[16 - 16 * h + k] = offr_ref[k]
    for b, first in enumerate((16 * h, 16 - 16 * h, 32 + 16 * h, 48 - 16 * h)):
        at = pl.multiple_of(4 * first, 64)
        for ref, row0, count in zip(blocks[3 * b : 3 * b + 3], (0, 24, 32), (24, 8, 24)):

            @pl.loop(0, count)
            def _(r, ref=ref, row0=row0, at=at):
                later[r + row0, pl.ds(at, 64), :] = ref[r].astype(F32)

    bin_id = lax.broadcasted_iota(jnp.int32, (32, 128), 0)

    @pl.loop(0, 4)
    def _(r8):
        for g in range(4):
            lane = pl.multiple_of(h * 512 + g * 128, 128)
            bins = bins_ref[pl.ds(pl.multiple_of(r8 * 8, 8), 8), pl.ds(lane, 128)]
            for i in range(8):
                at = pl.multiple_of(r8 * 1024 + i * 128, 128)
                hit = jnp.where(bins[i : i + 1] == bin_id, 1.0, 0.0)
                table[32 * g : 32 * g + 32, pl.ds(at, 128)] = hit.astype(BF16)

    low = lax.broadcasted_iota(jnp.int32, (8, 128), 0) < 4

    def one_row(r, carry):
        acc = [jnp.zeros((8, 128), F32) for _ in range(16)]
        for k in range(16):
            pair = later[r, 8 * k : 8 * k + 8, :]
            swap = pltpu.roll(pair, 4, 0)
            for odd in range(2):
                t = 2 * k + odd
                now = jnp.where(low, swap, pair) if odd else jnp.where(low, pair, swap)
                row = r + off[t]
                for j in range(16):
                    at = 4 * (t + 1 + 2 * j)
                    acc[j] = acc[j] + now * later[row, at : at + 8, :]
        at = pl.multiple_of(r * 128, 128)
        for j in range(8):
            two = jnp.concatenate([acc[2 * j], acc[2 * j + 1]], 0)
            high = two.astype(BF16)
            sums[16 * j : 16 * j + 16, pl.ds(at, 128)] = high
            rest = (two - high.astype(F32)).astype(BF16)
            sums[128 + 16 * j : 144 + 16 * j, pl.ds(at, 128)] = rest
        return carry

    lax.fori_loop(0, 32, one_row, 0)
    nt = (((1,), (1,)), ((), ()))
    both = lax.dot_general(sums[...], table[...], nt, preferred_element_type=F32)
    both = both[:128] + both[128:]
    row = lax.broadcasted_iota(jnp.int32, (128, 128), 0)
    col = lax.broadcasted_iota(jnp.int32, (128, 128), 1)
    both = jnp.where((row & 3) == (col >> 5), both, 0.0)
    q = lax.broadcasted_iota(jnp.int32, (32, 128), 0)
    lane = lax.broadcasted_iota(jnp.int32, (32, 128), 1)
    pick_q = jnp.where((lane & 31) == q, 1.0, 0.0)
    per_q = lax.dot_general(
        pick_q, both, nt, precision=lax.Precision.HIGHEST, preferred_element_type=F32
    )
    z = lax.broadcasted_iota(jnp.int32, (16, 128), 0)
    lane = lax.broadcasted_iota(jnp.int32, (16, 128), 1)
    for side in range(2):
        pick_l = jnp.where((lane >> 2) == 2 * z + side, 1.0, 0.0)
        part = lax.dot_general(
            per_q, pick_l, nt, precision=lax.Precision.HIGHEST, preferred_element_type=F32
        )
        for f in range(16):
            out_ref[2 * f + side] = part[2 * f : 2 * f + 2, :]


def correlate(h, off_own, off_other, bins, *blocks):
    return pl.pallas_call(
        correlate_kernel,
        out_shape=jax.ShapeDtypeStruct((32, 2, 16), F32),
        in_specs=[SMEM] * 3 + [VMEM] * 13,
        out_specs=VMEM,
        scratch_shapes=[
            pltpu.VMEM((56, 256, 128), F32),
            pltpu.VMEM((256, 4096), BF16),
            pltpu.VMEM((128, 4096), BF16),
            pltpu.SMEM((32,), jnp.int32),
        ],
        name="correlate",
        cost_estimate=pl.CostEstimate(flops=34000000, bytes_accessed=8000000, transcendentals=0),
        compiler_params=pltpu.CompilerParams(vmem_limit_bytes=24 << 20),
    )(h, off_own, off_other, bins, *blocks)


def per_device(frames, pixel_gain, couple, bin_index, pixel_mask, offsets):
    flow_count, time_count = lax.axis_size("flow"), lax.axis_size("tm")
    down = [(i, i + 1) for i in range(flow_count - 1)]
    up = [(i + 1, i) for i in range(flow_count - 1)]
    pair = [(i, i ^ 1) for i in range(time_count)]
    back = [(i + 2, i) for i in range(time_count - 2)]
    h = (lax.axis_index("tm") % 2).astype(jnp.int32).reshape(1)

    above = lax.ppermute(frames[:, 31, :], "flow", down)
    below = lax.ppermute(frames[:, 0, :], "flow", up)
    o24, o8, t24, t8 = correct(h, frames, above, below, pixel_gain, couple, pixel_mask)
    r24 = lax.ppermute(t24, "tm", pair)
    zo24 = lax.ppermute(o24, "tm", back)
    o_halo = lax.ppermute(o24, "flow", up)
    r8 = lax.ppermute(t8, "tm", pair)
    zo8 = lax.ppermute(o8, "tm", back)
    off_other = lax.ppermute(offsets, "tm", pair)
    r_halo = lax.ppermute(r24, "flow", up)
    zr24 = lax.ppermute(r24, "tm", back)
    zr8 = lax.ppermute(r8, "tm", back)
    zo_halo = lax.ppermute(zo24, "flow", up)
    zr_halo = lax.ppermute(zr24, "flow", up)
    part = correlate(
        h, offsets, off_other, bin_index,
        o24, o8, o_halo, r24, r8, r_halo, zo24, zo8, zo_halo, zr24, zr8, zr_halo,
    )
    both = ("flow", "tm")
    planes = [
        [f * time_count + 2 * z + s for f in range(flow_count) for s in range(2)]
        for z in range(time_count // 2)
    ]
    lines = [
        [f * time_count + 2 * z + s for z in range(time_count // 2)]
        for f in range(flow_count)
        for s in range(2)
    ]
    part = lax.all_to_all(part, both, 0, 0, axis_index_groups=planes).sum(0)
    part = lax.all_to_all(part.T.reshape(16, 1, 2), both, 0, 0, axis_index_groups=lines).sum(0)
    lag = (lax.axis_index("tm") + 1).astype(F32)
    normaliser = jnp.sqrt((16 * time_count - lag) * (32 * flow_count * 1024 / Q))
    return part.reshape(2, 1) / normaliser


def solution(mesh):
    in_specs = (
        P("tm", "flow", None),
        P("flow", None),
        P("flow", None),
        P("flow", None),
        P("flow", None),
        P("tm"),
    )
    return jax.shard_map(
        per_device, mesh=mesh, in_specs=in_specs, out_specs=P("flow", "tm"), check_vma=False
    )
```

```python
import jax
import jax.numpy as jnp
from jax import lax
from jax.experimental import pallas as pl
from jax.experimental.pallas import tpu as pltpu
from jax.sharding import PartitionSpec as P

LAGS = 32
OFF_MAX = 24
Q = 32
F32, BF16 = jnp.float32, jnp.bfloat16
VMEM = pl.BlockSpec(memory_space=pltpu.VMEM)
SMEM = pl.BlockSpec(memory_space=pltpu.SMEM)
NT = (((1,), (1,)), ((), ()))


def split_kernel(
    h_ref, f_ref, gain_ref, couple_ref, mask_ref, back, fwd, swap, up, down, coef, coef_up, work
):
    h = h_ref[0]

    @pl.loop(0, 16)
    def _(f):
        for j in range(8):
            cols = slice(128 * j, 128 * j + 128)
            start = (j // 4) * 2048 + (j % 4) + 4 * f
            for k in range(2):
                value = f_ref[f, 16 * k : 16 * k + 16, cols].astype(F32)
                work[pl.ds(start + 1024 * k, 8, stride=64), :] = value[:8]
                work[pl.ds(start + 1024 * k + 512, 8, stride=64), :] = value[8:]

    def row_of(half, r):
        return work[pl.ds(pl.multiple_of(half * 2048 + r * 64, 64), 64), :].astype(BF16)

    @pl.loop(0, 32)
    def _(r):
        back[r] = row_of(0, r)
        fwd[r] = row_of(1, r)
        swap[r] = row_of(1 - h, r)

    @pl.loop(0, 25)
    def _(r):
        up[r] = row_of(0, r)
        up[r + 25] = row_of(1, r)

    for half in range(2):
        down[half] = row_of(half, 31)
    for k in range(4):
        for j in range(8):
            rows, cols = slice(8 * k, 8 * k + 8), slice(128 * j, 128 * j + 128)
            good = mask_ref[rows, cols].astype(F32)
            at = pl.ds(32 * k + j % 4, 8, stride=4)
            for c, ref in enumerate((gain_ref, couple_ref)):
                value = ref[rows, cols] * good
                coef[c, j // 4, at, :] = value
                if k < 3:
                    coef_up[c, j // 4, at, :] = value


def split(h, frames, gain, couple, mask):
    block = lambda n: jax.ShapeDtypeStruct((n, 64, 128), BF16)
    return pl.pallas_call(
        split_kernel,
        out_shape=(
            block(32),
            block(32),
            block(32),
            block(50),
            block(2),
            jax.ShapeDtypeStruct((2, 2, 128, 128), F32),
            jax.ShapeDtypeStruct((2, 2, 96, 128), F32),
        ),
        in_specs=[SMEM] + [VMEM] * 4,
        out_specs=(VMEM,) * 7,
        scratch_shapes=[pltpu.VMEM((2 * 32 * 64, 128), F32)],
        name="split",
        cost_estimate=pl.CostEstimate(flops=1000000, bytes_accessed=3000000, transcendentals=0),
        compiler_params=pltpu.CompilerParams(vmem_limit_bytes=12 << 20),
    )(h, frames, gain, couple, mask)


def low_half():
    return lax.broadcasted_iota(jnp.int32, (8, 128), 0) < 4


def correct_rows(raw, coef, coef_up, half, count, put):
    low = low_half()

    def rows(k, source, at):
        pair = [source[c, half, pl.ds(pl.multiple_of(8 * at, 8), 8), :] for c in range(2)]
        swap = [pltpu.roll(v, 4, 0) for v in pair]
        line = [raw[2 * k + i].astype(F32) for i in range(4)]
        for odd in range(2):
            gain, couple = (
                jnp.where(low, s, v) if odd else jnp.where(low, v, s) for v, s in zip(pair, swap)
            )
            parts = []
            for i in range(8):
                at8 = slice(8 * i, 8 * i + 8)
                beside = line[odd][at8] + line[odd + 2][at8]
                parts.append(gain * line[odd + 1][at8] + couple * beside)
            put(2 * k + odd, jnp.concatenate(parts, 0).astype(BF16))

    @pl.loop(0, 16)
    def _(k):
        rows(k, coef, k)

    if count > 32:

        @pl.loop(16, count // 2)
        def _(k):
            rows(k, coef_up, k - 16)


def twice(pair, swap, odd, low):
    return jnp.where(low, swap, pair) if odd else jnp.where(low, pair, swap)


def own_kernel(
    h_ref, off_ref, bins_ref, half0, half1, above, below, coef, coef_up, fixed, acc_ref, table, raw, work
):
    h = h_ref[0]
    low = low_half()
    work[:, :, 64:72, :] = jnp.zeros((2, 56, 8, 128), F32)
    for half, main in enumerate((half0, half1)):
        raw[0] = above[half]

        @pl.loop(0, 32)
        def _(r, main=main):
            raw[r + 1] = main[r]

        @pl.loop(0, 25)
        def _(r, half=half):
            raw[r + 33] = below[25 * half + r]

        role = h if half == 0 else 1 - h

        def put(r, value, role=role):
            fixed[role, r] = value
            work[role, r, 0:64, :] = value.astype(F32)

        correct_rows(raw, coef, coef_up, half, 56, put)
    bin_id = lax.broadcasted_iota(jnp.int32, (32, 128), 0)
    for role in range(2):

        @pl.loop(0, 4)
        def _(r8, role=role):
            half = h if role == 0 else 1 - h
            for g in range(4):
                lane = pl.multiple_of(half * 512 + g * 128, 128)
                bins = bins_ref[pl.ds(pl.multiple_of(r8 * 8, 8), 8), pl.ds(lane, 128)]
                for i in range(8):
                    at = pl.multiple_of(role * 4096 + r8 * 1024 + i * 128, 128)
                    hit = jnp.where(bins[i : i + 1] == bin_id, 1.0, 0.0)
                    table[32 * g : 32 * g + 32, pl.ds(at, 128)] = hit.astype(BF16)

        @pl.loop(0, 32)
        def _(r, role=role):
            acc = [jnp.zeros((8, 128), F32) for _ in range(8)]
            for k in range(8):
                pair = work[role, r, 8 * k : 8 * k + 8, :]
                swap = pltpu.roll(pair, 4, 0)
                for odd in range(2):
                    t = 2 * k + odd
                    now = twice(pair, swap, odd, low)
                    row = r + off_ref[t]
                    for j in range((16 - t) // 2):
                        at = 4 * (t + 1 + 2 * j)
                        acc[j] = acc[j] + now * work[role, row, at : at + 8, :]
            for j in range(8):
                acc_ref[role, r, j] = acc[j]


def own_part(h, off, bins, half0, half1, above, below, coef, coef_up):
    return pl.pallas_call(
        own_kernel,
        out_shape=(
            jax.ShapeDtypeStruct((2, 56, 64, 128), BF16),
            jax.ShapeDtypeStruct((2, 32, 8, 8, 128), F32),
            jax.ShapeDtypeStruct((128, 8192), BF16),
        ),
        in_specs=[SMEM] * 2 + [VMEM] * 7,
        out_specs=(VMEM,) * 3,
        scratch_shapes=[pltpu.VMEM((58, 64, 128), BF16), pltpu.VMEM((2, 56, 72, 128), F32)],
        name="own",
        cost_estimate=pl.CostEstimate(flops=12000000, bytes_accessed=9000000, transcendentals=0),
        compiler_params=pltpu.CompilerParams(vmem_limit_bytes=20 << 20),
    )(h, off, bins, half0, half1, above, below, coef, coef_up)


def lag_kernel(
    h_ref, off_own, off_other, off_back, fixed, acc_ref, table, coef, coef_up,
    other, back, fwd, above, other_below, two_below, out_ref, raw, later, sums, off,
):
    h = h_ref[0]
    low = low_half()
    for k in range(16):
        off[48 * h + k] = off_own[k]
        off[16 + k] = off_other[k]
        off[48 - 48 * h + k] = off_back[k]
    at_own = [pl.multiple_of(128 * h, 64), pl.multiple_of(256 - 64 * h, 64)]
    at_back = pl.multiple_of(128 + 128 * h, 64)
    at_fwd = pl.multiple_of(192 - 192 * h, 64)
    later[:, 320:328, :] = jnp.zeros((56, 8, 128), F32)

    @pl.loop(0, 56)
    def _(r):
        for role in range(2):
            later[r, pl.ds(at_own[role], 64), :] = fixed[role, r].astype(F32)

    @pl.loop(32, 56)
    def _(r):
        later[r, pl.ds(at_fwd, 64), :] = jnp.zeros((64, 128), F32)

    for which, (main, half, count, at) in enumerate(
        ((other, h, 56, 64), (back, 0, 56, at_back), (fwd, 1, 32, at_fwd))
    ):
        raw[0] = above[which]

        @pl.loop(0, 32)
        def _(r, main=main):
            raw[r + 1] = main[r]

        if which == 2:
            raw[33] = two_below[25]
        else:
            below = two_below if which else other_below

            @pl.loop(0, 25)
            def _(r, below=below):
                raw[r + 33] = below[r]

        def put(r, value, at=at):
            later[r, pl.ds(at, 64), :] = value.astype(F32)

        correct_rows(raw, coef, coef_up, half, count, put)

    zero = jnp.zeros((8, 128), F32)

    def store(acc, at):
        at = pl.multiple_of(at, 128)
        for j in range(8):
            two = jnp.concatenate([acc[2 * j], acc[2 * j + 1]], 0)
            high = two.astype(BF16)
            sums[16 * j : 16 * j + 16, pl.ds(at, 128)] = high
            rest = (two - high.astype(F32)).astype(BF16)
            sums[128 + 16 * j : 144 + 16 * j, pl.ds(at, 128)] = rest

    def add_from(acc, r, source, target, off_at, first_lag, last_lag):
        for k in range(8):
            pair = later[r, source + 8 * k : source + 8 * k + 8, :]
            swap = pltpu.roll(pair, 4, 0)
            for odd in range(2):
                i = 2 * k + odd
                now = twice(pair, swap, odd, low)
                row = r + off[off_at + i]
                first, last = first_lag - i, last_lag(i)
                for j in range((first - 1) // 2, (last - 1) // 2 + 1):
                    x = now
                    if 2 * j + 1 < first:
                        x = jnp.where(low, 0.0, x)
                    if 2 * j + 2 > last:
                        x = jnp.where(low, x, 0.0)
                    at = target + 4 * (2 * j + 1 - first)
                    acc[j] = acc[j] + x * later[row, at : at + 8, :]

    @pl.loop(0, 32)
    def _(r):
        acc = [acc_ref[0, r, j] for j in range(8)] + [zero] * 8
        add_from(acc, r, 0, 64, 0, 16, lambda i: 32)
        add_from(acc, r, 64, 128, 16, 16, lambda i: 31 - i)
        store(acc, r * 128)
        acc = [acc_ref[1, r, j] for j in range(8)] + [zero] * 8
        add_from(acc, r, 192, 256, 48, 32, lambda i: 32)
        store(acc, 4096 + r * 128)

    both = lax.dot_general(sums[...], table[...], NT, preferred_element_type=F32)
    both = both[:128] + both[128:]
    row = lax.broadcasted_iota(jnp.int32, (128, 128), 0)
    col = lax.broadcasted_iota(jnp.int32, (128, 128), 1)
    both = jnp.where((row & 3) == (col >> 5), both, 0.0)
    q = lax.broadcasted_iota(jnp.int32, (32, 128), 0)
    lane = lax.broadcasted_iota(jnp.int32, (32, 128), 1)
    pick_q = jnp.where((lane & 31) == q, 1.0, 0.0)
    per_q = lax.dot_general(
        pick_q, both, NT, precision=lax.Precision.HIGHEST, preferred_element_type=F32
    )
    z = lax.broadcasted_iota(jnp.int32, (16, 128), 0)
    lane = lax.broadcasted_iota(jnp.int32, (16, 128), 1)
    for side in range(2):
        pick_l = jnp.where((lane >> 2) == 2 * z + side, 1.0, 0.0)
        part = lax.dot_general(
            per_q, pick_l, NT, precision=lax.Precision.HIGHEST, preferred_element_type=F32
        )
        for f in range(16):
            out_ref[2 * f + side] = part[2 * f : 2 * f + 2, :]


def lag_part(h, offs, fixed, acc, table, coef, coef_up, blocks):
    return pl.pallas_call(
        lag_kernel,
        out_shape=jax.ShapeDtypeStruct((32, 2, 16), F32),
        in_specs=[SMEM] * 4 + [VMEM] * 11,
        out_specs=VMEM,
        scratch_shapes=[
            pltpu.VMEM((58, 64, 128), BF16),
            pltpu.VMEM((56, 328, 128), F32),
            pltpu.VMEM((256, 8192), BF16),
            pltpu.SMEM((64,), jnp.int32),
        ],
        name="lags",
        cost_estimate=pl.CostEstimate(flops=34000000, bytes_accessed=12000000, transcendentals=0),
        compiler_params=pltpu.CompilerParams(vmem_limit_bytes=24 << 20),
    )(h, *offs, fixed, acc, table, coef, coef_up, *blocks)


def per_device(frames, pixel_gain, couple, bin_index, pixel_mask, offsets):
    flow_count, time_count = lax.axis_size("flow"), lax.axis_size("tm")
    down = [(i, i + 1) for i in range(flow_count - 1)]
    up = [(i + 1, i) for i in range(flow_count - 1)]
    pair = [(i, i ^ 1) for i in range(time_count)]
    backward = [(i + 2, i) for i in range(time_count - 2)]
    forward = [(i, i + 2) for i in range(time_count - 2)]
    h = (lax.axis_index("tm") % 2).astype(jnp.int32).reshape(1)

    half0, half1, swap, own_up, own_down, coef, coef_up = split(
        h, frames, pixel_gain, couple, pixel_mask
    )
    other = lax.ppermute(swap, "tm", pair)
    back = lax.ppermute(half0, "tm", backward)
    fwd = lax.ppermute(half1, "tm", forward)
    own_below = lax.ppermute(own_up, "flow", up)
    own_above = lax.ppermute(own_down, "flow", down)
    coef_below = lax.ppermute(coef_up, "flow", up)
    off_other = lax.ppermute(offsets, "tm", pair)
    off_back = lax.ppermute(offsets, "tm", forward)
    other_below = lax.ppermute(other[:25], "flow", up)
    two_below = lax.ppermute(jnp.concatenate([back[:25], fwd[:1]], 0), "flow", up)
    above = lax.ppermute(jnp.stack([other[31], back[31], fwd[31]]), "flow", down)
    fixed, acc, table = own_part(
        h, offsets, bin_index, half0, half1, own_above, own_below, coef, coef_below
    )
    part = lag_part(
        h, (offsets, off_other, off_back), fixed, acc, table, coef, coef_below,
        (other, back, fwd, above, other_below, two_below),
    )
    both = ("flow", "tm")
    planes = [
        [f * time_count + 2 * z + s for f in range(flow_count) for s in range(2)]
        for z in range(time_count // 2)
    ]
    lines = [
        [f * time_count + 2 * z + s for z in range(time_count // 2)]
        for f in range(flow_count)
        for s in range(2)
    ]
    lag = (lax.axis_index("tm") + 1).astype(F32)
    normaliser = jnp.sqrt((16 * time_count - lag) * (32 * flow_count * 1024 / Q))
    part, normaliser = lax.optimization_barrier((part, normaliser))
    part = lax.all_to_all(part, both, 0, 0, axis_index_groups=planes).sum(0)
    part = lax.all_to_all(part.T.reshape(16, 1, 2), both, 0, 0, axis_index_groups=lines).sum(0)
    return part.reshape(2, 1) / normaliser


def solution(mesh):
    in_specs = (
        P("tm", "flow", None),
        P("flow", None),
        P("flow", None),
        P("flow", None),
        P("flow", None),
        P("tm"),
    )
    return jax.shard_map(
        per_device, mesh=mesh, in_specs=in_specs, out_specs=P("flow", "tm"), check_vma=False
    )
```

```python
import jax
import jax.numpy as jnp
from jax import lax
from jax.experimental import pallas as pl
from jax.experimental.pallas import tpu as pltpu
from jax.sharding import PartitionSpec as P

OFF_MAX = 24
Q = 32
F32, BF16 = jnp.float32, jnp.bfloat16
VMEM = pl.BlockSpec(memory_space=pltpu.VMEM)
SMEM = pl.BlockSpec(memory_space=pltpu.SMEM)
HBM = pl.BlockSpec(memory_space=pltpu.HBM)
NT = (((1,), (1,)), ((), ()))


def correct_kernel(
    h_ref, off_ref, up_ref, dn_ref, f_hbm, gain_hbm, couple_hbm, mask_hbm,
    back, fwd, swap, own_up, raw, done, f_ref, gain_ref, couple_ref, mask_ref, sems,
):
    h = h_ref[0]
    pairs = (
        (f_hbm, f_ref), (gain_hbm, gain_ref), (couple_hbm, couple_ref), (mask_hbm, mask_ref)
    )
    copies = [pltpu.make_async_copy(a, b, sems.at[i]) for i, (a, b) in enumerate(pairs)]
    for copy in copies:
        copy.start()
    for copy in copies:
        copy.wait()

    @pl.loop(0, 16)
    def _(f):
        for j in range(8):
            cols = slice(128 * j, 128 * j + 128)
            for k in range(2):
                raw[f, j, 8 + 16 * k : 24 + 16 * k, :] = f_ref[
                    f, 16 * k : 16 * k + 16, cols
                ].astype(F32)

    for f in range(16):
        for j in range(8):
            cols = slice(128 * j, 128 * j + 128)
            raw[f, j, 7:8, :] = up_ref[f : f + 1, cols].astype(F32)
            raw[f, j, 40:41, :] = dn_ref[f : f + 1, cols].astype(F32)

    @pl.loop(0, 16)
    def _(f):
        for j in range(8):
            cols = slice(128 * j, 128 * j + 128)
            for k in range(4):
                rows = slice(8 * k, 8 * k + 8)
                here = raw[f, j, 8 * k + 8 : 8 * k + 16, :]
                above = raw[f, j, 8 * k + 7 : 8 * k + 15, :]
                below = raw[f, j, 8 * k + 9 : 8 * k + 17, :]
                value = gain_ref[rows, cols] * here + couple_ref[rows, cols] * (above + below)
                value = value * mask_ref[rows, cols].astype(F32)
                start = (j // 4) * 2048 + k * 512 + (j % 4) + 4 * f
                done[pl.ds(start, 8, stride=64), :] = value

    def row_of(half, r):
        return done[pl.ds(pl.multiple_of(half * 2048 + r * 64, 64), 64), :].astype(BF16)

    @pl.loop(0, 24)
    def _(r):
        first, second = row_of(0, r), row_of(1, r)
        back[r], fwd[r], swap[r] = first, second, row_of(1 - h, r)
        own_up[r], own_up[r + 24] = first, second

    @pl.loop(24, 32)
    def _(r):
        back[r], fwd[r], swap[r] = row_of(0, r), row_of(1, r), row_of(1 - h, r)

    frame = lax.broadcasted_iota(jnp.int32, (64, 128), 0) >> 2
    offs = jnp.zeros((64, 128), jnp.int32)
    for f in range(16):
        offs = jnp.where(frame == f, off_ref[f], offs)
    offs = offs.astype(F32).astype(BF16)
    fwd[32], swap[32] = offs, offs


def correct(h, off, frames, up, dn, gain, couple, mask):
    shapes = tuple(jax.ShapeDtypeStruct((n, 64, 128), BF16) for n in (32, 33, 33, 48))
    return pl.pallas_call(
        correct_kernel,
        out_shape=shapes,
        in_specs=[SMEM] * 2 + [VMEM] * 2 + [HBM] * 4,
        out_specs=(VMEM,) * 4,
        scratch_shapes=[
            pltpu.VMEM((16, 8, 48, 128), F32),
            pltpu.VMEM((2 * 32 * 64, 128), F32),
            pltpu.VMEM((16, 32, 1024), BF16),
            pltpu.VMEM((32, 1024), F32),
            pltpu.VMEM((32, 1024), F32),
            pltpu.VMEM((32, 1024), jnp.int32),
            pltpu.SemaphoreType.DMA((4,)),
        ],
        name="correct",
        cost_estimate=pl.CostEstimate(flops=4000000, bytes_accessed=3000000, transcendentals=0),
        compiler_params=pltpu.CompilerParams(vmem_limit_bytes=63100 << 10),
    )(h, off, up, dn, frames, gain, couple, mask)


def low_half():
    return lax.broadcasted_iota(jnp.int32, (8, 128), 0) < 4


def twice(pair, swap, odd, low):
    return jnp.where(low, swap, pair) if odd else jnp.where(low, pair, swap)


def table_kernel(h_ref, bins_ref, table):
    h = h_ref[0]
    bin_id = lax.broadcasted_iota(jnp.int32, (32, 128), 0)
    for role in range(2):

        @pl.loop(0, 4)
        def _(r8, role=role):
            half = h if role == 0 else 1 - h
            for g in range(4):
                lane = pl.multiple_of(half * 512 + g * 128, 128)
                bins = bins_ref[pl.ds(pl.multiple_of(r8 * 8, 8), 8), pl.ds(lane, 128)]
                for i in range(8):
                    at = pl.multiple_of(role * 4096 + r8 * 1024 + i * 128, 128)
                    hit = jnp.where(bins[i : i + 1] == bin_id, 1.0, 0.0)
                    table[32 * g : 32 * g + 32, pl.ds(at, 128)] = hit.astype(BF16)


def bin_table(h, bins):
    return pl.pallas_call(
        table_kernel,
        out_shape=jax.ShapeDtypeStruct((128, 8192), BF16),
        in_specs=[SMEM, VMEM],
        out_specs=VMEM,
        name="table",
        cost_estimate=pl.CostEstimate(flops=1000000, bytes_accessed=2000000, transcendentals=0),
        compiler_params=pltpu.CompilerParams(vmem_limit_bytes=6 << 20),
    )(h, bins)


def own_kernel(
    h_ref, off_ref, half0, half1, below, acc_ref, work
):
    h = h_ref[0]
    low = low_half()
    work[:, :, 64:72, :] = jnp.zeros((2, 56, 8, 128), F32)
    for half, main in enumerate((half0, half1)):
        role = h if half == 0 else 1 - h

        @pl.loop(0, 32)
        def _(r, main=main, role=role):
            work[role, r, 0:64, :] = main[r].astype(F32)

        @pl.loop(0, 24)
        def _(r, half=half, role=role):
            work[role, r + 32, 0:64, :] = below[24 * half + r].astype(F32)

    for role in range(2):

        @pl.loop(0, 32)
        def _(r, role=role):
            acc = [jnp.zeros((8, 128), F32) for _ in range(8)]
            for k in range(8):
                pair = work[role, r, 8 * k : 8 * k + 8, :]
                swap = pltpu.roll(pair, 4, 0)
                for odd in range(2):
                    t = 2 * k + odd
                    now = twice(pair, swap, odd, low)
                    row = r + off_ref[t]
                    for j in range((16 - t) // 2):
                        at = 4 * (t + 1 + 2 * j)
                        acc[j] = acc[j] + now * work[role, row, at : at + 8, :]
            for j in range(8):
                acc_ref[role, r, j] = acc[j]


def own_part(h, off, half0, half1, below):
    return pl.pallas_call(
        own_kernel,
        out_shape=jax.ShapeDtypeStruct((2, 32, 8, 8, 128), F32),
        in_specs=[SMEM] * 2 + [VMEM] * 3,
        out_specs=VMEM,
        scratch_shapes=[pltpu.VMEM((2, 56, 72, 128), F32)],
        name="own",
        cost_estimate=pl.CostEstimate(flops=8000000, bytes_accessed=7000000, transcendentals=0),
        compiler_params=pltpu.CompilerParams(vmem_limit_bytes=20 << 20),
    )(h, off, half0, half1, below)


def pack_kernel(other, back, two):
    @pl.loop(0, 24)
    def _(r):
        two[r] = other[r]
        two[r + 24] = back[r]


def pack(other, back):
    return pl.pallas_call(
        pack_kernel,
        out_shape=jax.ShapeDtypeStruct((48, 64, 128), BF16),
        in_specs=[VMEM] * 2,
        out_specs=VMEM,
        name="pack",
        cost_estimate=pl.CostEstimate(flops=0, bytes_accessed=1600000, transcendentals=0),
        compiler_params=pltpu.CompilerParams(vmem_limit_bytes=4 << 20),
    )(other, back)


def add_from(acc, later, off, r, source, target, off_at, first_lag, last_lag):
    low = low_half()
    for k in range(8):
        pair = later[r, source + 8 * k : source + 8 * k + 8, :]
        swap = pltpu.roll(pair, 4, 0)
        for odd in range(2):
            i = 2 * k + odd
            now = twice(pair, swap, odd, low)
            row = r + off[off_at + i]
            first, last = first_lag - i, last_lag(i)
            for j in range((first - 1) // 2, (last - 1) // 2 + 1):
                x = now
                if 2 * j + 1 < first:
                    x = jnp.where(low, 0.0, x)
                if 2 * j + 2 > last:
                    x = jnp.where(low, x, 0.0)
                at = target + 4 * (2 * j + 1 - first)
                acc[j] = acc[j] + x * later[row, at : at + 8, :]


def all_lags(later, off, acc_ref, sums, r, at, rows):
    zero = jnp.zeros((8, 128), F32)

    def store(acc, at):
        at = pl.multiple_of(at, 128)
        for j in range(8):
            two = jnp.concatenate([acc[2 * j], acc[2 * j + 1]], 0)
            high = two.astype(BF16)
            sums[16 * j : 16 * j + 16, pl.ds(at, 128)] = high
            rest = (two - high.astype(F32)).astype(BF16)
            sums[128 + 16 * j : 144 + 16 * j, pl.ds(at, 128)] = rest

    acc = [acc_ref[0, r, j] for j in range(8)] + [zero] * 8
    add_from(acc, later, off, r, 0, 64, 0, 16, lambda i: 32)
    add_from(acc, later, off, r, 64, 128, 16, 16, lambda i: 31 - i)
    store(acc, at)
    acc = [acc_ref[1, r, j] for j in range(8)] + [zero] * 8
    add_from(acc, later, off, r, 192, 256, 48, 32, lambda i: 32)
    store(acc, rows * 128 + at)


EARLY = 32 - OFF_MAX


def early_kernel(
    h_ref, off_own, acc_ref, half0, half1, own_below, other, back, fwd,
    later, sums, off, off_rows, off_read, sem,
):
    h = h_ref[0]
    off_rows[0] = other[32].astype(F32).astype(jnp.int32)
    off_rows[1] = fwd[32].astype(F32).astype(jnp.int32)
    read = pltpu.make_async_copy(off_rows, off_read, sem)
    read.start()
    at_half = [pl.multiple_of(192 * h, 64), pl.multiple_of(256 - 128 * h, 64)]
    at_back = pl.multiple_of(128 + 128 * h, 64)
    at_fwd = pl.multiple_of(192 - 192 * h, 64)
    later[:, 320:328, :] = jnp.zeros((56, 8, 128), F32)

    @pl.loop(0, 32)
    def _(r):
        later[r, pl.ds(at_half[0], 64), :] = half0[r].astype(F32)
        later[r, pl.ds(at_half[1], 64), :] = half1[r].astype(F32)
        later[r, 64:128, :] = other[r].astype(F32)
        later[r, pl.ds(at_back, 64), :] = back[r].astype(F32)
        later[r, pl.ds(at_fwd, 64), :] = fwd[r].astype(F32)

    @pl.loop(0, 24)
    def _(r):
        later[r + 32, pl.ds(at_half[0], 64), :] = own_below[r].astype(F32)
        later[r + 32, pl.ds(at_half[1], 64), :] = own_below[r + 24].astype(F32)
        later[r + 32, pl.ds(at_fwd, 64), :] = jnp.zeros((64, 128), F32)

    read.wait()
    for k in range(16):
        off[48 * h + k] = off_own[k]
        off[16 + k] = off_read[0, 4 * k, 0]
        off[48 - 48 * h + k] = off_read[1, 4 * k, 0]

    @pl.loop(0, EARLY)
    def _(r):
        all_lags(later, off, acc_ref, sums, r, r * 128, EARLY)


def early_part(h, off, acc, blocks):
    return pl.pallas_call(
        early_kernel,
        out_shape=(
            jax.ShapeDtypeStruct((56, 328, 128), F32),
            jax.ShapeDtypeStruct((256, 2 * EARLY * 128), BF16),
            jax.ShapeDtypeStruct((64,), jnp.int32),
        ),
        in_specs=[SMEM] * 2 + [VMEM] * 7,
        out_specs=(VMEM, VMEM, SMEM),
        scratch_shapes=[
            pltpu.VMEM((2, 64, 128), jnp.int32),
            pltpu.SMEM((2, 64, 128), jnp.int32),
            pltpu.SemaphoreType.DMA,
        ],
        name="early",
        cost_estimate=pl.CostEstimate(flops=8000000, bytes_accessed=12000000, transcendentals=0),
        compiler_params=pltpu.CompilerParams(vmem_limit_bytes=16 << 20),
    )(h, off, acc, *blocks)


def late_kernel(h_ref, off, later_in, acc_ref, table, sums_early, two_below, later, out_ref, sums):
    h = h_ref[0]
    at_back = pl.multiple_of(128 + 128 * h, 64)

    @pl.loop(0, 24)
    def _(r):
        later[r + 32, 64:128, :] = two_below[r].astype(F32)
        later[r + 32, pl.ds(at_back, 64), :] = two_below[r + 24].astype(F32)

    rows = 32 - EARLY

    @pl.loop(EARLY, 32)
    def _(r):
        all_lags(later, off, acc_ref, sums, r, (r - EARLY) * 128, rows)

    both = jnp.zeros((256, 128), F32)
    for role in range(2):
        for ref, first, count in ((sums_early, 0, EARLY), (sums, EARLY, rows)):
            left = ref[:, role * count * 128 : (role + 1) * count * 128]
            start = role * 4096 + first * 128
            right = table[:, start : start + count * 128]
            both = both + lax.dot_general(left, right, NT, preferred_element_type=F32)
    both = both[:128] + both[128:]
    row = lax.broadcasted_iota(jnp.int32, (128, 128), 0)
    col = lax.broadcasted_iota(jnp.int32, (128, 128), 1)
    both = jnp.where((row & 3) == (col >> 5), both, 0.0)
    q = lax.broadcasted_iota(jnp.int32, (32, 128), 0)
    lane = lax.broadcasted_iota(jnp.int32, (32, 128), 1)
    pick_q = jnp.where((lane & 31) == q, 1.0, 0.0)
    per_q = lax.dot_general(
        pick_q, both, NT, precision=lax.Precision.HIGHEST, preferred_element_type=F32
    )
    z = lax.broadcasted_iota(jnp.int32, (16, 128), 0)
    lane = lax.broadcasted_iota(jnp.int32, (16, 128), 1)
    for side in range(2):
        pick_l = jnp.where((lane >> 2) == 2 * z + side, 1.0, 0.0)
        part = lax.dot_general(
            per_q, pick_l, NT, precision=lax.Precision.HIGHEST, preferred_element_type=F32
        )
        for f in range(16):
            out_ref[2 * f + side] = part[2 * f : 2 * f + 2, :]


def late_part(h, off, later, acc, table, sums, two_below):
    return pl.pallas_call(
        late_kernel,
        out_shape=(
            jax.ShapeDtypeStruct((56, 328, 128), F32),
            jax.ShapeDtypeStruct((32, 2, 16), F32),
        ),
        in_specs=[SMEM] * 2 + [VMEM] * 5,
        out_specs=(VMEM,) * 2,
        input_output_aliases={2: 0},
        scratch_shapes=[pltpu.VMEM((256, 2 * (32 - EARLY) * 128), BF16)],
        name="late",
        cost_estimate=pl.CostEstimate(flops=24000000, bytes_accessed=12000000, transcendentals=0),
        compiler_params=pltpu.CompilerParams(vmem_limit_bytes=16 << 20),
    )(h, off, later, acc, table, sums, two_below)[1]


def device_program(frames, pixel_gain, couple, bin_index, pixel_mask, offsets):
    flow_count, time_count = lax.axis_size("flow"), lax.axis_size("tm")
    down = [(i, i + 1) for i in range(flow_count - 1)]
    up = [(i + 1, i) for i in range(flow_count - 1)]
    pair = [(i, i ^ 1) for i in range(time_count)]
    backward = [(i + 2, i) for i in range(time_count - 2)]
    forward = [(i, i + 2) for i in range(time_count - 2)]
    h = (lax.axis_index("tm") % 2).astype(jnp.int32).reshape(1)

    above = lax.ppermute(frames[:, 31, :], "flow", down)
    below = lax.ppermute(frames[:, 0, :], "flow", up)
    half0, half1, swap, own_up = correct(
        h, offsets, frames, above, below, pixel_gain, couple, pixel_mask
    )
    table = bin_table(h, bin_index)
    other = lax.ppermute(swap, "tm", pair)
    back = lax.ppermute(half0, "tm", backward)
    fwd = lax.ppermute(half1, "tm", forward)
    own_below = lax.ppermute(own_up, "flow", up)
    acc = own_part(h, offsets, half0, half1, own_below)
    two_below = lax.ppermute(pack(other, back), "flow", up)
    later, sums, off = early_part(
        h, offsets, acc, (half0, half1, own_below, other, back, fwd)
    )
    part = late_part(h, off, later, acc, table, sums, two_below)
    both = ("flow", "tm")
    planes = [
        [f * time_count + 2 * z + s for f in range(flow_count) for s in range(2)]
        for z in range(time_count // 2)
    ]
    lines = [
        [f * time_count + 2 * z + s for z in range(time_count // 2)]
        for f in range(flow_count)
        for s in range(2)
    ]
    lag = (lax.axis_index("tm") + 1).astype(F32)
    normaliser = jnp.sqrt((16 * time_count - lag) * (32 * flow_count * 1024 / Q))
    part, normaliser = lax.optimization_barrier((part, normaliser))
    part = lax.all_to_all(part, both, 0, 0, axis_index_groups=planes).sum(0)
    part = lax.all_to_all(part.T.reshape(16, 1, 2), both, 0, 0, axis_index_groups=lines).sum(0)
    return part.reshape(2, 1) / normaliser


def solution(mesh):
    in_specs = (
        P("tm", "flow", None),
        P("flow", None),
        P("flow", None),
        P("flow", None),
        P("flow", None),
        P("tm"),
    )
    return jax.shard_map(
        device_program, mesh=mesh, in_specs=in_specs, out_specs=P("flow", "tm"), check_vma=False
    )
```

```python
import functools

import jax
import jax.numpy as jnp
from jax import lax
from jax.experimental import pallas as pl
from jax.experimental.pallas import tpu as pltpu
from jax.sharding import PartitionSpec as P

OFF_MAX = 24
Q = 32
F32, BF16 = jnp.float32, jnp.bfloat16
VMEM = pl.BlockSpec(memory_space=pltpu.VMEM)
SMEM = pl.BlockSpec(memory_space=pltpu.SMEM)
NT = (((1,), (1,)), ((), ()))


def correct_kernel(
    off_ref, f_ref, up_ref, dn_ref, gain_ref, couple_ref, mask_ref,
    back, fwd, swap, own_up, raw, done,
):
    h = lax.rem(lax.axis_index("tm"), 2)

    @pl.loop(0, 16)
    def _(f):
        for j in range(8):
            cols = slice(128 * j, 128 * j + 128)
            for k in range(2):
                raw[f, j, 8 + 16 * k : 24 + 16 * k, :] = f_ref[
                    f, 16 * k : 16 * k + 16, cols
                ].astype(F32)

    for f in range(16):
        for j in range(8):
            cols = slice(128 * j, 128 * j + 128)
            raw[f, j, 7:8, :] = up_ref[f : f + 1, cols].astype(F32)
            raw[f, j, 40:41, :] = dn_ref[f : f + 1, cols].astype(F32)

    @pl.loop(0, 16)
    def _(f):
        for j in range(8):
            cols = slice(128 * j, 128 * j + 128)
            for k in range(4):
                rows = slice(8 * k, 8 * k + 8)
                here = raw[f, j, 8 * k + 8 : 8 * k + 16, :]
                above = raw[f, j, 8 * k + 7 : 8 * k + 15, :]
                below = raw[f, j, 8 * k + 9 : 8 * k + 17, :]
                value = gain_ref[rows, cols] * here + couple_ref[rows, cols] * (above + below)
                value = value * mask_ref[rows, cols].astype(F32)
                start = (j // 4) * 2048 + k * 512 + (j % 4) + 4 * f
                done[pl.ds(start, 8, stride=64), :] = value

    def row_of(half, r):
        return done[pl.ds(pl.multiple_of(half * 2048 + r * 64, 64), 64), :].astype(BF16)

    @pl.loop(0, 24)
    def _(r):
        first, second = row_of(0, r), row_of(1, r)
        back[r], fwd[r], swap[r] = first, second, row_of(1 - h, r)
        own_up[r], own_up[r + 24] = first, second

    @pl.loop(24, 32)
    def _(r):
        back[r], fwd[r], swap[r] = row_of(0, r), row_of(1, r), row_of(1 - h, r)

    frame = lax.broadcasted_iota(jnp.int32, (64, 128), 0) >> 2
    offs = jnp.zeros((64, 128), jnp.int32)
    for f in range(16):
        offs = jnp.where(frame == f, off_ref[f], offs)
    offs = offs.astype(F32).astype(BF16)
    fwd[32], swap[32] = offs, offs


def correct(off, frames, up, dn, gain, couple, mask):
    shapes = tuple(jax.ShapeDtypeStruct((n, 64, 128), BF16) for n in (32, 33, 33, 48))
    return pl.pallas_call(
        correct_kernel,
        out_shape=shapes,
        in_specs=[SMEM] + [VMEM] * 6,
        out_specs=(VMEM,) * 4,
        scratch_shapes=[
            pltpu.VMEM((16, 8, 48, 128), F32),
            pltpu.VMEM((2 * 32 * 64, 128), F32),
        ],
        name="correct",
        cost_estimate=pl.CostEstimate(flops=4000000, bytes_accessed=3000000, transcendentals=0),
        compiler_params=pltpu.CompilerParams(vmem_limit_bytes=12 << 20),
    )(off, frames, up, dn, gain, couple, mask)


def low_half():
    return lax.broadcasted_iota(jnp.int32, (8, 128), 0) < 4


def twice(pair, swap, odd, low):
    return jnp.where(low, swap, pair) if odd else jnp.where(low, pair, swap)


def table_kernel(role, bins_ref, table):
    h = lax.rem(lax.axis_index("tm"), 2)
    half = h if role == 0 else 1 - h
    bin_id = lax.broadcasted_iota(jnp.int32, (32, 128), 0)

    @pl.loop(0, 4)
    def _(r8):
        for g in range(4):
            lane = pl.multiple_of(half * 512 + g * 128, 128)
            bins = bins_ref[pl.ds(pl.multiple_of(r8 * 8, 8), 8), pl.ds(lane, 128)]
            for i in range(8):
                at = pl.multiple_of(r8 * 1024 + i * 128, 128)
                hit = jnp.where(bins[i : i + 1] == bin_id, 1.0, 0.0)
                table[32 * g : 32 * g + 32, pl.ds(at, 128)] = hit.astype(BF16)


def bin_table(role, bins, cost):
    return pl.pallas_call(
        functools.partial(table_kernel, role),
        out_shape=jax.ShapeDtypeStruct((128, 4096), BF16),
        in_specs=[VMEM],
        out_specs=VMEM,
        name="table",
        cost_estimate=pl.CostEstimate(flops=cost, bytes_accessed=2000000, transcendentals=0),
        compiler_params=pltpu.CompilerParams(vmem_limit_bytes=4 << 20),
    )(bins)


def own_lags(half0, half1, below, off, acc_ref, work):
    h = lax.rem(lax.axis_index("tm"), 2)
    low = low_half()
    work[:, :, 64:72, :] = jnp.zeros((2, 56, 8, 128), F32)
    for half, main in enumerate((half0, half1)):
        role = h if half == 0 else 1 - h

        @pl.loop(0, 32)
        def _(r, main=main, role=role):
            work[role, r, 0:64, :] = main[r].astype(F32)

        @pl.loop(0, 24)
        def _(r, half=half, role=role):
            work[role, r + 32, 0:64, :] = below[24 * half + r].astype(F32)

    for role in range(2):

        @pl.loop(0, 32)
        def _(r, role=role):
            acc = [jnp.zeros((8, 128), F32) for _ in range(8)]
            for k in range(8):
                pair = work[role, r, 8 * k : 8 * k + 8, :]
                swap = pltpu.roll(pair, 4, 0)
                for odd in range(2):
                    t = 2 * k + odd
                    now = twice(pair, swap, odd, low)
                    row = r + off[48 * h + t]
                    for j in range((16 - t) // 2):
                        at = 4 * (t + 1 + 2 * j)
                        acc[j] = acc[j] + now * work[role, row, at : at + 8, :]
            for j in range(8):
                acc_ref[role, r, j] = acc[j]


def pack_kernel(other, back, two):
    @pl.loop(0, 24)
    def _(r):
        two[r] = other[r]
        two[r + 24] = back[r]


def pack(other, back):
    return pl.pallas_call(
        pack_kernel,
        out_shape=jax.ShapeDtypeStruct((48, 64, 128), BF16),
        in_specs=[VMEM] * 2,
        out_specs=VMEM,
        name="pack",
        cost_estimate=pl.CostEstimate(flops=0, bytes_accessed=1600000, transcendentals=0),
        compiler_params=pltpu.CompilerParams(vmem_limit_bytes=4 << 20),
    )(other, back)


def add_from(acc, later, off, r, source, target, off_at, first_lag, last_lag):
    low = low_half()
    for k in range(8):
        pair = later[r, source + 8 * k : source + 8 * k + 8, :]
        swap = pltpu.roll(pair, 4, 0)
        for odd in range(2):
            i = 2 * k + odd
            now = twice(pair, swap, odd, low)
            row = r + off[off_at + i]
            first, last = first_lag - i, last_lag(i)
            for j in range((first - 1) // 2, (last - 1) // 2 + 1):
                x = now
                if 2 * j + 1 < first:
                    x = jnp.where(low, 0.0, x)
                if 2 * j + 2 > last:
                    x = jnp.where(low, x, 0.0)
                at = target + 4 * (2 * j + 1 - first)
                acc[j] = acc[j] + x * later[row, at : at + 8, :]


def all_lags(later, off, acc_ref, sums, r, at, rows):
    zero = jnp.zeros((8, 128), F32)

    def store(acc, at):
        at = pl.multiple_of(at, 128)
        for j in range(8):
            two = jnp.concatenate([acc[2 * j], acc[2 * j + 1]], 0)
            high = two.astype(BF16)
            sums[16 * j : 16 * j + 16, pl.ds(at, 128)] = high
            rest = (two - high.astype(F32)).astype(BF16)
            sums[128 + 16 * j : 144 + 16 * j, pl.ds(at, 128)] = rest

    acc = [acc_ref[0, r, j] for j in range(8)] + [zero] * 8
    add_from(acc, later, off, r, 0, 64, 0, 16, lambda i: 32)
    add_from(acc, later, off, r, 64, 128, 16, 16, lambda i: 31 - i)
    store(acc, at)
    acc = [acc_ref[1, r, j] for j in range(8)] + [zero] * 8
    add_from(acc, later, off, r, 192, 256, 48, 32, lambda i: 32)
    store(acc, rows * 128 + at)


EARLY = 32 - OFF_MAX


def early_kernel(
    half0, half1, own_below, other, back, fwd,
    acc_ref, later, sums, off, off_rows, off_read, work, sem,
):
    h = lax.rem(lax.axis_index("tm"), 2)
    off_rows[0] = other[32].astype(F32).astype(jnp.int32)
    off_rows[1] = fwd[32].astype(F32).astype(jnp.int32)
    off_rows[2] = half1[32].astype(F32).astype(jnp.int32)
    read = pltpu.make_async_copy(off_rows, off_read, sem)
    read.start()
    at_half = [pl.multiple_of(192 * h, 64), pl.multiple_of(256 - 128 * h, 64)]
    at_back = pl.multiple_of(128 + 128 * h, 64)
    at_fwd = pl.multiple_of(192 - 192 * h, 64)
    later[:, 320:328, :] = jnp.zeros((56, 8, 128), F32)

    @pl.loop(0, 32)
    def _(r):
        later[r, pl.ds(at_half[0], 64), :] = half0[r].astype(F32)
        later[r, pl.ds(at_half[1], 64), :] = half1[r].astype(F32)
        later[r, 64:128, :] = other[r].astype(F32)
        later[r, pl.ds(at_back, 64), :] = back[r].astype(F32)
        later[r, pl.ds(at_fwd, 64), :] = fwd[r].astype(F32)

    @pl.loop(0, 24)
    def _(r):
        later[r + 32, pl.ds(at_half[0], 64), :] = own_below[r].astype(F32)
        later[r + 32, pl.ds(at_half[1], 64), :] = own_below[r + 24].astype(F32)
        later[r + 32, pl.ds(at_fwd, 64), :] = jnp.zeros((64, 128), F32)

    read.wait()
    for k in range(16):
        off[48 * h + k] = off_read[2, 4 * k, 0]
        off[16 + k] = off_read[0, 4 * k, 0]
        off[48 - 48 * h + k] = off_read[1, 4 * k, 0]

    own_lags(half0, half1, own_below, off, acc_ref, work)

    @pl.loop(0, EARLY)
    def _(r):
        all_lags(later, off, acc_ref, sums, r, r * 128, EARLY)


def early_part(blocks):
    return pl.pallas_call(
        early_kernel,
        out_shape=(
            jax.ShapeDtypeStruct((2, 32, 8, 8, 128), F32),
            jax.ShapeDtypeStruct((56, 328, 128), F32),
            jax.ShapeDtypeStruct((256, 2 * EARLY * 128), BF16),
            jax.ShapeDtypeStruct((64,), jnp.int32),
        ),
        in_specs=[VMEM] * 6,
        out_specs=(VMEM, VMEM, VMEM, SMEM),
        scratch_shapes=[
            pltpu.VMEM((3, 64, 128), jnp.int32),
            pltpu.SMEM((3, 64, 128), jnp.int32),
            pltpu.VMEM((2, 56, 72, 128), F32),
            pltpu.SemaphoreType.DMA,
        ],
        name="early",
        cost_estimate=pl.CostEstimate(flops=16000000, bytes_accessed=16000000, transcendentals=0),
        compiler_params=pltpu.CompilerParams(vmem_limit_bytes=8 << 20),
    )(*blocks)


def late_kernel(
    frames_total, pixels_per_bin,
    off, later_in, acc_ref, table0, table1, sums_early, two_below, later, out_ref, sums,
):
    h = lax.rem(lax.axis_index("tm"), 2)
    at_back = pl.multiple_of(128 + 128 * h, 64)

    @pl.loop(0, 24)
    def _(r):
        later[r + 32, 64:128, :] = two_below[r].astype(F32)
        later[r + 32, pl.ds(at_back, 64), :] = two_below[r + 24].astype(F32)

    rows = 32 - EARLY

    @pl.loop(EARLY, 32)
    def _(r):
        all_lags(later, off, acc_ref, sums, r, (r - EARLY) * 128, rows)

    both = jnp.zeros((256, 128), F32)
    for role in range(2):
        for ref, first, count in ((sums_early, 0, EARLY), (sums, EARLY, rows)):
            left = ref[:, role * count * 128 : (role + 1) * count * 128]
            right = (table0, table1)[role][:, first * 128 : (first + count) * 128]
            both = both + lax.dot_general(left, right, NT, preferred_element_type=F32)
    both = both[:128] + both[128:]
    row = lax.broadcasted_iota(jnp.int32, (128, 128), 0)
    col = lax.broadcasted_iota(jnp.int32, (128, 128), 1)
    both = jnp.where((row & 3) == (col >> 5), both, 0.0)
    q = lax.broadcasted_iota(jnp.int32, (32, 128), 0)
    lane = lax.broadcasted_iota(jnp.int32, (32, 128), 1)
    pick_q = jnp.where((lane & 31) == q, 1.0, 0.0)
    per_q = lax.dot_general(
        pick_q, both, NT, precision=lax.Precision.HIGHEST, preferred_element_type=F32
    )
    z = lax.broadcasted_iota(jnp.int32, (16, 128), 0)
    lane = lax.broadcasted_iota(jnp.int32, (16, 128), 1)
    for side in range(2):
        pick_l = jnp.where((lane >> 2) == 2 * z + side, 1.0, 0.0)
        part = lax.dot_general(
            per_q, pick_l, NT, precision=lax.Precision.HIGHEST, preferred_element_type=F32
        )
        lag = (2 * lax.broadcasted_iota(jnp.int32, (32, 16), 1) + side + 1).astype(F32)
        part = part / jnp.sqrt((frames_total - lag) * pixels_per_bin)
        for f in range(16):
            out_ref[2 * f + side] = part[2 * f : 2 * f + 2, :]


def late_part(totals, off, later, acc, table, sums, two_below):
    return pl.pallas_call(
        functools.partial(late_kernel, *totals),
        out_shape=(
            jax.ShapeDtypeStruct((56, 328, 128), F32),
            jax.ShapeDtypeStruct((32, 2, 16), F32),
        ),
        in_specs=[SMEM] + [VMEM] * 6,
        out_specs=(VMEM,) * 2,
        input_output_aliases={1: 0},
        scratch_shapes=[pltpu.VMEM((256, 2 * (32 - EARLY) * 128), BF16)],
        name="late",
        cost_estimate=pl.CostEstimate(flops=24000000, bytes_accessed=12000000, transcendentals=0),
        compiler_params=pltpu.CompilerParams(vmem_limit_bytes=8 << 20),
    )(off, later, acc, *table, sums, two_below)[1]


def device_program(frames, pixel_gain, couple, bin_index, pixel_mask, offsets):
    flow_count, time_count = lax.axis_size("flow"), lax.axis_size("tm")
    down = [(i, i + 1) for i in range(flow_count - 1)]
    up = [(i + 1, i) for i in range(flow_count - 1)]
    pair = [(i, i ^ 1) for i in range(time_count)]
    backward = [(i + 2, i) for i in range(time_count - 2)]
    forward = [(i, i + 2) for i in range(time_count - 2)]

    above = lax.ppermute(frames[:, 31, :], "flow", down)
    below = lax.ppermute(frames[:, 0, :], "flow", up)
    half0, half1, swap, own_up = correct(
        offsets, frames, above, below, pixel_gain, couple, pixel_mask
    )
    table0 = bin_table(0, bin_index, 12000000000)
    table1 = bin_table(1, bin_index, 1000000)
    other = lax.ppermute(swap, "tm", pair)
    back = lax.ppermute(half0, "tm", backward)
    fwd = lax.ppermute(half1, "tm", forward)
    own_below = lax.ppermute(own_up, "flow", up)
    two_below = lax.ppermute(pack(other, back), "flow", up)
    acc, later, sums, off = early_part((half0, half1, own_below, other, back, fwd))
    totals = (16 * time_count, 32 * flow_count * 1024 / Q)
    part = late_part(totals, off, later, acc, (table0, table1), sums, two_below)
    both = ("flow", "tm")
    planes = [
        [f * time_count + 2 * z + s for f in range(flow_count) for s in range(2)]
        for z in range(time_count // 2)
    ]
    lines = [
        [f * time_count + 2 * z + s for z in range(time_count // 2)]
        for f in range(flow_count)
        for s in range(2)
    ]
    part = lax.all_to_all(part, both, 0, 0, axis_index_groups=planes).sum(0)
    part = lax.all_to_all(part.T.reshape(16, 1, 2), both, 0, 0, axis_index_groups=lines).sum(0)
    return part.reshape(2, 1)


def solution(mesh):
    in_specs = (
        P("tm", "flow", None),
        P("flow", None),
        P("flow", None),
        P("flow", None),
        P("flow", None),
        P("tm"),
    )
    return jax.shard_map(
        device_program, mesh=mesh, in_specs=in_specs, out_specs=P("flow", "tm"), check_vma=False
    )
```

```python
import functools

import jax
import jax.numpy as jnp
from jax import lax
from jax.experimental import pallas as pl
from jax.experimental.pallas import tpu as pltpu
from jax.sharding import PartitionSpec as P

OFF_MAX = 24
Q = 32
F32, BF16 = jnp.float32, jnp.bfloat16
VMEM = pl.BlockSpec(memory_space=pltpu.VMEM)
SMEM = pl.BlockSpec(memory_space=pltpu.SMEM)
NT = (((1,), (1,)), ((), ()))


def split_kernel(off_ref, f_ref, back, fwd, swap, up, down, work):
    h = lax.rem(lax.axis_index("tm"), 2)

    @pl.loop(0, 16)
    def _(f):
        for j in range(8):
            cols = slice(128 * j, 128 * j + 128)
            start = (j // 4) * 2048 + (j % 4) + 4 * f
            for k in range(2):
                value = f_ref[f, 16 * k : 16 * k + 16, cols].astype(F32)
                work[pl.ds(start + 1024 * k, 8, stride=64), :] = value[:8]
                work[pl.ds(start + 1024 * k + 512, 8, stride=64), :] = value[8:]

    def row_of(half, r):
        return work[pl.ds(pl.multiple_of(half * 2048 + r * 64, 64), 64), :].astype(BF16)

    @pl.loop(0, 25)
    def _(r):
        first, second = row_of(0, r), row_of(1, r)
        back[r], fwd[r], swap[r] = first, second, row_of(1 - h, r)
        up[r], up[r + 25] = first, second

    @pl.loop(25, 32)
    def _(r):
        back[r], fwd[r], swap[r] = row_of(0, r), row_of(1, r), row_of(1 - h, r)

    for half in range(2):
        down[half] = row_of(half, 31)
    frame = lax.broadcasted_iota(jnp.int32, (64, 128), 0) >> 2
    offs = jnp.zeros((64, 128), jnp.int32)
    for f in range(16):
        offs = jnp.where(frame == f, off_ref[f], offs)
    offs = offs.astype(F32).astype(BF16)
    fwd[32], swap[32] = offs, offs


def split(off, frames):
    return pl.pallas_call(
        split_kernel,
        out_shape=tuple(jax.ShapeDtypeStruct((n, 64, 128), BF16) for n in (32, 33, 33, 50, 2)),
        in_specs=[SMEM, VMEM],
        out_specs=(VMEM,) * 5,
        scratch_shapes=[pltpu.VMEM((2 * 32 * 64, 128), F32)],
        name="split",
        cost_estimate=pl.CostEstimate(flops=12000000000, bytes_accessed=3000000, transcendentals=0),
        compiler_params=pltpu.CompilerParams(vmem_limit_bytes=8 << 20),
    )(off, frames)


def coef_kernel(gain_ref, couple_ref, mask_ref, coef, coef_up):
    for k in range(4):
        for j in range(8):
            rows, cols = slice(8 * k, 8 * k + 8), slice(128 * j, 128 * j + 128)
            good = mask_ref[rows, cols].astype(F32)
            at = pl.ds(32 * k + j % 4, 8, stride=4)
            for c, ref in enumerate((gain_ref, couple_ref)):
                value = ref[rows, cols] * good
                coef[c, j // 4, at, :] = value
                if k < 3:
                    coef_up[c, j // 4, at, :] = value


def masked_coef(gain, couple, mask):
    return pl.pallas_call(
        coef_kernel,
        out_shape=(
            jax.ShapeDtypeStruct((2, 2, 128, 128), F32),
            jax.ShapeDtypeStruct((2, 2, 96, 128), F32),
        ),
        in_specs=[VMEM] * 3,
        out_specs=(VMEM,) * 2,
        name="coef",
        cost_estimate=pl.CostEstimate(flops=1000000, bytes_accessed=1000000, transcendentals=0),
        compiler_params=pltpu.CompilerParams(vmem_limit_bytes=4 << 20),
    )(gain, couple, mask)


def low_half():
    return lax.broadcasted_iota(jnp.int32, (8, 128), 0) < 4


def twice(pair, swap, odd, low):
    return jnp.where(low, swap, pair) if odd else jnp.where(low, pair, swap)


def correct_pair(raw, source, at, half, k, put):
    low = low_half()
    pair = [source[c, half, pl.ds(pl.multiple_of(8 * at, 8), 8), :] for c in range(2)]
    swap = [pltpu.roll(v, 4, 0) for v in pair]
    line = [raw[2 * k + i].astype(F32) for i in range(4)]
    for odd in range(2):
        gain, couple = (twice(v, s, odd, low) for v, s in zip(pair, swap))
        parts = []
        for i in range(8):
            at8 = slice(8 * i, 8 * i + 8)
            beside = line[odd][at8] + line[odd + 2][at8]
            parts.append(gain * line[odd + 1][at8] + couple * beside)
        put(2 * k + odd, jnp.concatenate(parts, 0).astype(BF16).astype(F32))


def stage_rows(raw, main):
    @pl.loop(0, 32)
    def _(r):
        raw[r + 1] = main[r]


def table_kernel(role, bins_ref, table):
    h = lax.rem(lax.axis_index("tm"), 2)
    half = h if role == 0 else 1 - h
    bin_id = lax.broadcasted_iota(jnp.int32, (32, 128), 0)

    @pl.loop(0, 4)
    def _(r8):
        for g in range(4):
            lane = pl.multiple_of(half * 512 + g * 128, 128)
            bins = bins_ref[pl.ds(pl.multiple_of(r8 * 8, 8), 8), pl.ds(lane, 128)]
            for i in range(8):
                at = pl.multiple_of(r8 * 1024 + i * 128, 128)
                hit = jnp.where(bins[i : i + 1] == bin_id, 1.0, 0.0)
                table[32 * g : 32 * g + 32, pl.ds(at, 128)] = hit.astype(BF16)


def bin_table(role, bins, cost):
    return pl.pallas_call(
        functools.partial(table_kernel, role),
        out_shape=jax.ShapeDtypeStruct((128, 4096), BF16),
        in_specs=[VMEM],
        out_specs=VMEM,
        name="table",
        cost_estimate=pl.CostEstimate(flops=cost, bytes_accessed=2000000, transcendentals=0),
        compiler_params=pltpu.CompilerParams(vmem_limit_bytes=4 << 20),
    )(bins)


def own_lags(off, acc_ref, work):
    h = lax.rem(lax.axis_index("tm"), 2)
    low = low_half()
    for role in range(2):

        @pl.loop(0, 32)
        def _(r, role=role):
            acc = [jnp.zeros((8, 128), F32) for _ in range(8)]
            for k in range(8):
                pair = work[role, r, 8 * k : 8 * k + 8, :]
                swap = pltpu.roll(pair, 4, 0)
                for odd in range(2):
                    t = 2 * k + odd
                    now = twice(pair, swap, odd, low)
                    row = r + off[48 * h + t]
                    for j in range((16 - t) // 2):
                        at = 4 * (t + 1 + 2 * j)
                        acc[j] = acc[j] + now * work[role, row, at : at + 8, :]
            for j in range(8):
                acc_ref[role, r, j] = acc[j]


def pack_kernel(other, back, fwd, two, three):
    @pl.loop(0, 25)
    def _(r):
        two[r] = other[r]
        two[r + 25] = back[r]

    two[50] = fwd[0]
    for i, ref in enumerate((other, back, fwd)):
        three[i] = ref[31]


def pack(other, back, fwd):
    return pl.pallas_call(
        pack_kernel,
        out_shape=tuple(jax.ShapeDtypeStruct((n, 64, 128), BF16) for n in (51, 3)),
        in_specs=[VMEM] * 3,
        out_specs=(VMEM,) * 2,
        name="pack",
        cost_estimate=pl.CostEstimate(flops=0, bytes_accessed=1600000, transcendentals=0),
        compiler_params=pltpu.CompilerParams(vmem_limit_bytes=4 << 20),
    )(other, back, fwd)


def add_from(acc, later, off, r, source, target, off_at, first_lag, last_lag):
    low = low_half()
    for k in range(8):
        pair = later[r, source + 8 * k : source + 8 * k + 8, :]
        swap = pltpu.roll(pair, 4, 0)
        for odd in range(2):
            i = 2 * k + odd
            now = twice(pair, swap, odd, low)
            row = r + off[off_at + i]
            first, last = first_lag - i, last_lag(i)
            for j in range((first - 1) // 2, (last - 1) // 2 + 1):
                x = now
                if 2 * j + 1 < first:
                    x = jnp.where(low, 0.0, x)
                if 2 * j + 2 > last:
                    x = jnp.where(low, x, 0.0)
                at = target + 4 * (2 * j + 1 - first)
                acc[j] = acc[j] + x * later[row, at : at + 8, :]


def all_lags(later, off, acc_ref, sums, r, at, rows):
    zero = jnp.zeros((8, 128), F32)

    def store(acc, at):
        at = pl.multiple_of(at, 128)
        for j in range(8):
            two = jnp.concatenate([acc[2 * j], acc[2 * j + 1]], 0)
            high = two.astype(BF16)
            sums[16 * j : 16 * j + 16, pl.ds(at, 128)] = high
            rest = (two - high.astype(F32)).astype(BF16)
            sums[128 + 16 * j : 144 + 16 * j, pl.ds(at, 128)] = rest

    acc = [acc_ref[0, r, j] for j in range(8)] + [zero] * 8
    add_from(acc, later, off, r, 0, 64, 0, 16, lambda i: 32)
    add_from(acc, later, off, r, 64, 128, 16, 16, lambda i: 31 - i)
    store(acc, at)
    acc = [acc_ref[1, r, j] for j in range(8)] + [zero] * 8
    add_from(acc, later, off, r, 192, 256, 48, 32, lambda i: 32)
    store(acc, rows * 128 + at)


FIRST, LAST = 1, 31 - OFF_MAX
EARLY = LAST - FIRST


def early_kernel(
    half0, half1, own_above, own_below, coef, coef_up, other, back, fwd,
    acc_ref, later, sums, off, off_rows, off_read, work, raw, sem,
):
    h = lax.rem(lax.axis_index("tm"), 2)
    off_rows[0] = other[32].astype(F32).astype(jnp.int32)
    off_rows[1] = fwd[32].astype(F32).astype(jnp.int32)
    off_rows[2] = half1[32].astype(F32).astype(jnp.int32)
    read = pltpu.make_async_copy(off_rows, off_read, sem)
    read.start()
    at_half = [pl.multiple_of(192 * h, 64), pl.multiple_of(256 - 128 * h, 64)]
    at_back = pl.multiple_of(128 + 128 * h, 64)
    at_fwd = pl.multiple_of(192 - 192 * h, 64)
    later[:, 320:328, :] = jnp.zeros((56, 8, 128), F32)
    work[:, :, 64:72, :] = jnp.zeros((2, 56, 8, 128), F32)

    @pl.loop(32, 56)
    def _(r):
        later[r, pl.ds(at_fwd, 64), :] = jnp.zeros((64, 128), F32)

    for half, main in enumerate((half0, half1)):
        role = h if half == 0 else 1 - h
        raw[0] = own_above[half]
        stage_rows(raw, main)

        @pl.loop(0, 25)
        def _(r, half=half):
            raw[r + 33] = own_below[25 * half + r]

        def put(r, value, half=half, role=role):
            later[r, pl.ds(at_half[half], 64), :] = value
            work[role, r, 0:64, :] = value

        @pl.loop(0, 16)
        def _(k, half=half, put=put):
            correct_pair(raw, coef, k, half, k, put)

        @pl.loop(16, 28)
        def _(k, half=half, put=put):
            correct_pair(raw, coef_up, k - 16, half, k, put)

    for main, half, at in ((other, h, 64), (back, 0, at_back), (fwd, 1, at_fwd)):
        raw[0], raw[33] = main[0], main[0]
        stage_rows(raw, main)

        def put(r, value, at=at):
            later[r, pl.ds(at, 64), :] = value

        @pl.loop(0, 16)
        def _(k, half=half, put=put):
            correct_pair(raw, coef, k, half, k, put)

    read.wait()
    for k in range(16):
        off[48 * h + k] = off_read[2, 4 * k, 0]
        off[16 + k] = off_read[0, 4 * k, 0]
        off[48 - 48 * h + k] = off_read[1, 4 * k, 0]

    own_lags(off, acc_ref, work)

    @pl.loop(FIRST, LAST)
    def _(r):
        all_lags(later, off, acc_ref, sums, r, (r - FIRST) * 128, EARLY)


def early_part(blocks):
    return pl.pallas_call(
        early_kernel,
        out_shape=(
            jax.ShapeDtypeStruct((2, 32, 8, 8, 128), F32),
            jax.ShapeDtypeStruct((56, 328, 128), F32),
            jax.ShapeDtypeStruct((256, 2 * EARLY * 128), BF16),
            jax.ShapeDtypeStruct((64,), jnp.int32),
        ),
        in_specs=[VMEM] * 9,
        out_specs=(VMEM, VMEM, VMEM, SMEM),
        scratch_shapes=[
            pltpu.VMEM((3, 64, 128), jnp.int32),
            pltpu.SMEM((3, 64, 128), jnp.int32),
            pltpu.VMEM((2, 56, 72, 128), F32),
            pltpu.VMEM((58, 64, 128), BF16),
            pltpu.SemaphoreType.DMA,
        ],
        name="early",
        cost_estimate=pl.CostEstimate(flops=16000000, bytes_accessed=16000000, transcendentals=0),
        compiler_params=pltpu.CompilerParams(vmem_limit_bytes=8 << 20),
    )(*blocks)


def late_kernel(
    frames_total, pixels_per_bin,
    off, later_in, acc_ref, table0, table1, sums_early, coef, coef_up, other, back, fwd,
    two_below, above, later, out_ref, sums, raw,
):
    h = lax.rem(lax.axis_index("tm"), 2)
    at_back = pl.multiple_of(128 + 128 * h, 64)
    at_fwd = pl.multiple_of(192 - 192 * h, 64)
    for which, (main, half, at) in enumerate(((other, h, 64), (back, 0, at_back), (fwd, 1, at_fwd))):
        raw[0] = above[which]
        stage_rows(raw, main)

        def put(r, value, at=at):
            later[r, pl.ds(at, 64), :] = value

        if which < 2:

            @pl.loop(0, 25)
            def _(r, which=which):
                raw[r + 33] = two_below[25 * which + r]

            @pl.loop(16, 28)
            def _(k, half=half, put=put):
                correct_pair(raw, coef_up, k - 16, half, k, put)

        else:
            raw[33] = two_below[50]
        correct_pair(raw, coef, 0, half, 0, put)
        correct_pair(raw, coef, 15, half, 15, put)

    rows = 32 - EARLY
    all_lags(later, off, acc_ref, sums, 0, 0, rows)

    @pl.loop(LAST, 32)
    def _(r):
        all_lags(later, off, acc_ref, sums, r, (r - EARLY) * 128, rows)

    both = jnp.zeros((256, 128), F32)
    for role in range(2):
        table = (table0, table1)[role]
        for ref, at, first, count in (
            (sums_early, role * EARLY, FIRST, EARLY),
            (sums, role * rows, 0, FIRST),
            (sums, role * rows + FIRST, LAST, 32 - LAST),
        ):
            left = ref[:, at * 128 : (at + count) * 128]
            right = table[:, first * 128 : (first + count) * 128]
            both = both + lax.dot_general(left, right, NT, preferred_element_type=F32)
    both = both[:128] + both[128:]
    row = lax.broadcasted_iota(jnp.int32, (128, 128), 0)
    col = lax.broadcasted_iota(jnp.int32, (128, 128), 1)
    both = jnp.where((row & 3) == (col >> 5), both, 0.0)
    q = lax.broadcasted_iota(jnp.int32, (32, 128), 0)
    lane = lax.broadcasted_iota(jnp.int32, (32, 128), 1)
    pick_q = jnp.where((lane & 31) == q, 1.0, 0.0)
    per_q = lax.dot_general(
        pick_q, both, NT, precision=lax.Precision.HIGHEST, preferred_element_type=F32
    )
    z = lax.broadcasted_iota(jnp.int32, (16, 128), 0)
    lane = lax.broadcasted_iota(jnp.int32, (16, 128), 1)
    for side in range(2):
        pick_l = jnp.where((lane >> 2) == 2 * z + side, 1.0, 0.0)
        part = lax.dot_general(
            per_q, pick_l, NT, precision=lax.Precision.HIGHEST, preferred_element_type=F32
        )
        lag = (2 * lax.broadcasted_iota(jnp.int32, (32, 16), 1) + side + 1).astype(F32)
        part = part / jnp.sqrt((frames_total - lag) * pixels_per_bin)
        for f in range(16):
            out_ref[2 * f + side] = part[2 * f : 2 * f + 2, :]


def late_part(totals, off, later, acc, table, sums, rest):
    return pl.pallas_call(
        functools.partial(late_kernel, *totals),
        out_shape=(
            jax.ShapeDtypeStruct((56, 328, 128), F32),
            jax.ShapeDtypeStruct((32, 2, 16), F32),
        ),
        in_specs=[SMEM] + [VMEM] * 12,
        out_specs=(VMEM,) * 2,
        input_output_aliases={1: 0},
        scratch_shapes=[
            pltpu.VMEM((256, 2 * (32 - EARLY) * 128), BF16),
            pltpu.VMEM((58, 64, 128), BF16),
        ],
        name="late",
        cost_estimate=pl.CostEstimate(flops=24000000, bytes_accessed=12000000, transcendentals=0),
        compiler_params=pltpu.CompilerParams(vmem_limit_bytes=8 << 20),
    )(off, later, acc, *table, sums, *rest)[1]


def device_program(frames, pixel_gain, couple, bin_index, pixel_mask, offsets):
    flow_count, time_count = lax.axis_size("flow"), lax.axis_size("tm")
    down = [(i, i + 1) for i in range(flow_count - 1)]
    up = [(i + 1, i) for i in range(flow_count - 1)]
    pair = [(i, i ^ 1) for i in range(time_count)]
    backward = [(i + 2, i) for i in range(time_count - 2)]
    forward = [(i, i + 2) for i in range(time_count - 2)]

    table0 = bin_table(0, bin_index, 1000000)
    table1 = bin_table(1, bin_index, 1000000)
    half0, half1, swap, own_up, own_down = split(offsets, frames)
    coef, coef_up = masked_coef(pixel_gain, couple, pixel_mask)
    other = lax.ppermute(swap, "tm", pair)
    back = lax.ppermute(half0, "tm", backward)
    fwd = lax.ppermute(half1, "tm", forward)
    own_below = lax.ppermute(own_up, "flow", up)
    own_above = lax.ppermute(own_down, "flow", down)
    coef_below = lax.ppermute(coef_up, "flow", up)
    two, three = pack(other, back, fwd)
    two_below = lax.ppermute(two, "flow", up)
    above = lax.ppermute(three, "flow", down)
    acc, later, sums, off = early_part(
        (half0, half1, own_above, own_below, coef, coef_below, other, back, fwd)
    )
    totals = (16 * time_count, 32 * flow_count * 1024 / Q)
    part = late_part(
        totals, off, later, acc, (table0, table1), sums,
        (coef, coef_below, other, back, fwd, two_below, above),
    )
    both = ("flow", "tm")
    planes = [
        [f * time_count + 2 * z + s for f in range(flow_count) for s in range(2)]
        for z in range(time_count // 2)
    ]
    lines = [
        [f * time_count + 2 * z + s for z in range(time_count // 2)]
        for f in range(flow_count)
        for s in range(2)
    ]
    part = lax.all_to_all(part, both, 0, 0, axis_index_groups=planes).sum(0)
    part = lax.all_to_all(part.T.reshape(16, 1, 2), both, 0, 0, axis_index_groups=lines).sum(0)
    return part.reshape(2, 1)


def solution(mesh):
    in_specs = (
        P("tm", "flow", None),
        P("flow", None),
        P("flow", None),
        P("flow", None),
        P("flow", None),
        P("tm"),
    )
    return jax.shard_map(
        device_program, mesh=mesh, in_specs=in_specs, out_specs=P("flow", "tm"), check_vma=False
    )
```
